32 devices in a mesh: fsdp: 2 (over x), ctx: 16 (over z, y, core).
Axes of the slice: x: 2, y: 2, z: 4, core: 2. Of those that a mesh axis runs over, the one named last changes fastest.
Arguments:
- inputs: bfloat16 [2, 2048, 960], P('fsdp', 'ctx'), may hold values from -6 to 6
- grad_output: bfloat16 [2, 2048, 960], P('fsdp', 'ctx'), may hold values from -6 to 6
- w_query: bfloat16 [960, 960], P('fsdp', 'ctx'), may hold values from -50 to 50
- w_key: bfloat16 [960, 320], P('fsdp', 'ctx'), may hold values from -50 to 50
- w_value: bfloat16 [960, 320], P('fsdp', 'ctx'), may hold values from -0.1875 to 0.1875
- w_out: bfloat16 [960, 960], P('fsdp', 'ctx'), may hold values from -0.75 to 0.75
- w_gate: bfloat16 [960, 2560], P('fsdp', 'ctx'), may hold values from -0.1875 to 0.1875
- w_up: bfloat16 [960, 2560], P('fsdp', 'ctx'), may hold values from -0.1875 to 0.1875
- w_down: bfloat16 [2560, 960], P('fsdp', 'ctx'), may hold values from -0.125 to 0.125
- gain_attn: bfloat16 [960], P('ctx'), may hold values from 0.5 to 1.5
- gain_mlp: bfloat16 [960], P('ctx'), may hold values from 0.5 to 1.5
Outputs:
- output: bfloat16 [2, 2048, 960], P('fsdp', 'ctx')
- grad_input: bfloat16 [2, 2048, 960], P('fsdp', 'ctx')
- grad_w_query: float32 [960, 960], P('fsdp', 'ctx')
- grad_w_key: float32 [960, 320], P('fsdp', 'ctx')
- grad_w_value: float32 [960, 320], P('fsdp', 'ctx')
- grad_w_out: float32 [960, 960], P('fsdp', 'ctx')
- grad_w_gate: float32 [960, 2560], P('fsdp', 'ctx')
- grad_w_up: float32 [960, 2560], P('fsdp', 'ctx')
- grad_w_down: float32 [2560, 960], P('fsdp', 'ctx')
- grad_gain_attn: float32 [960], P('ctx')
- grad_gain_mlp: float32 [960], P('ctx')
The draws below stay inside these ranges and needn't reach their ends.
All inputs are finite; a program needn't handle non-finite values.
Results may differ from the reference program's by a relative error of at most 0.018.
Values may be sent and summed in bfloat16 or wider, within the bound.
A program may use at most 256 MiB of HBM per device.

```python
import math
import jax
import jax.numpy as jnp
from jax import lax

D = 960
FF = 2560
HEADS = 15
KV_HEADS = 5
HEAD = 64
SEQS = 2
LENGTH = 2048
KEY_BLOCK = 512


def paired_weights(key):
    base_key = jax.random.fold_in(key, 71)
    subkeys = jax.random.split(base_key, 3)
    key_matrix = jax.random.normal(subkeys[0], (D, KV_HEADS * HEAD), jnp.float32) / math.sqrt(D)
    query_matrix = jax.random.normal(subkeys[2], (D, HEADS * HEAD), jnp.float32) / math.sqrt(D)
    return (query_matrix, key_matrix)


def draw_w_query(key, part):
    query_matrix, key_matrix = paired_weights(key)
    return query_matrix.astype(jnp.bfloat16)


def draw_w_key(key, part):
    query_matrix, key_matrix = paired_weights(key)
    return key_matrix.astype(jnp.bfloat16)


def level_of(own_key, dims, cuts, low, top_value):
    loudness, own = 1.0, jax.random.fold_in(own_key, 6)
    for dim, shards_of in cuts:
        steps = jnp.exp(jax.random.uniform(jax.random.fold_in(own, dim), (shards_of,), jnp.float32, low / len(cuts), top_value / len(cuts)))
        loudness = loudness * jnp.repeat(steps, dims[dim] // shards_of).reshape([-1 if axis == dim else 1 for axis in range(len(dims))])
    return loudness


def bell_draw(rng, shape, width, bound, cuts=(), held_as=jnp.bfloat16):
    result = width * jax.random.normal(rng, shape, jnp.float32)
    if cuts:
        result = result * level_of(rng, shape, cuts, -0.22, 0.18)
    return jnp.clip(result, -bound, bound).astype(held_as)


def setup_inputs(seed: int = 0) -> dict:
    splits = jax.random.split(jax.random.key(seed), 12)
    return {
        "inputs": bell_draw(splits[0], (SEQS, LENGTH, D), 1.0, 6.0, ((0, 2), (1, 16))),
        "grad_output": bell_draw(splits[1], (SEQS, LENGTH, D), 1.0, 6.0, ((0, 2), (1, 16))),
        "w_query": draw_w_query(jax.random.fold_in(splits[11], 71), 0),
        "w_key": draw_w_key(jax.random.fold_in(splits[11], 71), 0),
        "w_value": bell_draw(splits[4], (D, KV_HEADS * HEAD), D ** -0.5, 0.1875, ((0, 2), (1, 16))),
        "w_out": bell_draw(splits[5], (HEADS * HEAD, D), 64 ** -0.5, 0.75, ((0, 2), (1, 16))),
        "w_gate": bell_draw(splits[6], (D, FF), D ** -0.5, 0.1875, ((0, 2), (1, 16))),
        "w_up": bell_draw(splits[7], (D, FF), D ** -0.5, 0.1875, ((0, 2), (1, 16))),
        "w_down": bell_draw(splits[8], (FF, D), FF ** -0.5, 0.125, ((0, 2), (1, 16))),
        "gain_attn": jnp.clip(1.0 + 0.1 * jax.random.normal(splits[9], (D,), jnp.float32), 0.5, 1.5).astype(jnp.bfloat16),
        "gain_mlp": jnp.clip(1.0 + 0.1 * jax.random.normal(splits[10], (D,), jnp.float32), 0.5, 1.5).astype(jnp.bfloat16),
    }


EPSILON = 1e-05
ROPE_THETA = 100000.0

def lowered(tensor):
    return lax.optimization_barrier(tensor.astype(jnp.bfloat16)).astype(jnp.float32)

def tables(positions, head_size):
    half_size = head_size // 2
    frequency = ROPE_THETA ** (-jnp.arange(half_size, dtype=jnp.float32) * 2.0 / head_size)
    angles = positions.astype(jnp.float32)[:, None] * frequency[None, :]
    return (jnp.cos(angles), jnp.sin(angles))

def rotate(values, cosine, sine_table):
    half_size = values.shape[-1] // 2
    first_half = values[..., :half_size]
    second = values[..., half_size:]
    cosine = cosine[:, None, :]
    sine_table = sine_table[:, None, :]
    return jnp.concatenate([first_half * cosine - second * sine_table, second * cosine + first_half * sine_table], axis=-1)

def unrotate(values, cosine, sine_table):
    half_size = values.shape[-1] // 2
    first_half = values[..., :half_size]
    second = values[..., half_size:]
    cosine = cosine[:, None, :]
    sine_table = sine_table[:, None, :]
    return jnp.concatenate([first_half * cosine + second * sine_table, second * cosine - first_half * sine_table], axis=-1)

def normed(row_values, gain_vec):
    scale_rows = lax.rsqrt(lax.optimization_barrier(jnp.mean(row_values * row_values, axis=-1, keepdims=True)) + EPSILON)
    return row_values * scale_rows * gain_vec

def attention_forward(query_rot, key_rows, value_rows):
    block_total = LENGTH // KEY_BLOCK
    key_pos = jnp.arange(LENGTH, dtype=jnp.int32)

    def query_block(block_index):
        row_start = block_index * KEY_BLOCK
        query_rows = lax.dynamic_slice_in_dim(query_rot, row_start, KEY_BLOCK, 0)
        scores = jnp.einsum('qgrd,kgd->grqk', query_rows.astype(jnp.float32), key_rows.astype(jnp.float32)) * 0.125
        allowed = key_pos[None, :] <= (row_start + jnp.arange(KEY_BLOCK, dtype=jnp.int32))[:, None]
        scores = jnp.where(allowed, scores, -jnp.inf)
        new_peak = lax.optimization_barrier(jnp.max(scores, axis=-1))
        logsum = new_peak + jnp.log(lax.optimization_barrier(jnp.sum(jnp.exp(scores - new_peak[..., None]), axis=-1)))
        prob_low = lowered(jnp.exp(scores - logsum[..., None]))
        attended = jnp.einsum('grqk,kgd->qgrd', prob_low, value_rows.astype(jnp.float32)).astype(jnp.bfloat16)
        return (attended, logsum)
    attended, logsum = lax.map(query_block, jnp.arange(block_total, dtype=jnp.int32))
    return (attended.reshape(LENGTH, KV_HEADS, HEADS // KV_HEADS, HEAD), logsum)

def attention_backward(query_rot, key_rows, value_rows, attended, logsum, grad_attended):
    block_total = LENGTH // KEY_BLOCK
    key_pos = jnp.arange(LENGTH, dtype=jnp.int32)

    def query_block(loop_state, block_index):
        grad_keys, grad_values = loop_state
        row_start = block_index * KEY_BLOCK
        query_rows = lax.dynamic_slice_in_dim(query_rot, row_start, KEY_BLOCK, 0).astype(jnp.float32)
        grad_rows = lax.dynamic_slice_in_dim(grad_attended, row_start, KEY_BLOCK, 0).astype(jnp.float32)
        scores = jnp.einsum('qgrd,kgd->grqk', query_rows, key_rows.astype(jnp.float32)) * 0.125
        allowed = key_pos[None, :] <= (row_start + jnp.arange(KEY_BLOCK, dtype=jnp.int32))[:, None]
        scores = jnp.where(allowed, scores, -jnp.inf)
        prob_full = jnp.where(allowed, jnp.exp(scores - logsum[block_index][..., None]), 0.0)
        grad_probs = jnp.einsum('qgrd,kgd->grqk', grad_rows, value_rows.astype(jnp.float32))
        row_delta = lax.optimization_barrier(jnp.sum(prob_full * grad_probs, axis=-1))
        grad_scores = lowered(prob_full * (grad_probs - row_delta[..., None]) * 0.125)
        grad_values = grad_values + jnp.einsum('grqk,qgrd->kgd', lowered(prob_full), grad_rows)
        grad_keys = grad_keys + jnp.einsum('grqk,qgrd->kgd', grad_scores, query_rows)
        grad_query = jnp.einsum('grqk,kgd->qgrd', grad_scores, key_rows.astype(jnp.float32))
        return ((grad_keys, grad_values), grad_query)
    zero_sums = (jnp.zeros((LENGTH, KV_HEADS, HEAD), jnp.float32), jnp.zeros((LENGTH, KV_HEADS, HEAD), jnp.float32))
    (grad_keys, grad_values), grad_query = lax.scan(query_block, zero_sums, jnp.arange(block_total, dtype=jnp.int32))
    return (grad_query.reshape(LENGTH, HEADS, HEAD), grad_keys, grad_values)

def one_sequence(rows_in, grad_rows, weights, gains):
    full_query, full_key, full_value, full_out, full_gate, full_up, full_down = weights
    gain_first, gain_second = gains
    repeat_count = HEADS // KV_HEADS
    cosine, sine_table = tables(jnp.arange(LENGTH, dtype=jnp.int32), HEAD)
    resid1 = rows_in.astype(jnp.float32)
    normal1 = normed(resid1, gain_first).astype(jnp.bfloat16)
    query_raw = jnp.dot(normal1, full_query, preferred_element_type=jnp.float32).reshape(LENGTH, HEADS, HEAD)
    query_rot = rotate(query_raw, cosine, sine_table).astype(jnp.bfloat16)
    key_raw = jnp.dot(normal1, full_key, preferred_element_type=jnp.float32).reshape(LENGTH, KV_HEADS, HEAD)
    key_rows = rotate(key_raw, cosine, sine_table).astype(jnp.bfloat16)
    value_rows = jnp.dot(normal1, full_value, preferred_element_type=jnp.float32).astype(jnp.bfloat16).reshape(LENGTH, KV_HEADS, HEAD)
    query_grouped = query_rot.reshape(LENGTH, KV_HEADS, repeat_count, HEAD)
    attended, logsum = attention_forward(query_grouped, key_rows, value_rows)
    attended_rows = attended.reshape(LENGTH, HEADS * HEAD)
    resid2 = resid1 + jnp.dot(attended_rows, full_out, preferred_element_type=jnp.float32)
    normal2 = normed(resid2, gain_second).astype(jnp.bfloat16)
    gate_act = jnp.dot(normal2, full_gate, preferred_element_type=jnp.float32)
    up_act = jnp.dot(normal2, full_up, preferred_element_type=jnp.float32)
    hidden = (jax.nn.silu(gate_act) * up_act).astype(jnp.bfloat16)
    output = (resid2 + jnp.dot(hidden, full_down, preferred_element_type=jnp.float32)).astype(jnp.bfloat16)
    grad_hidden = jnp.dot(grad_rows, full_down.T, preferred_element_type=jnp.float32)
    term_down = jnp.dot(hidden.T, grad_rows, preferred_element_type=jnp.float32)
    gate_sigma = jax.nn.sigmoid(gate_act)
    grad_up = (grad_hidden * gate_act * gate_sigma).astype(jnp.bfloat16)
    grad_gate = (grad_hidden * up_act * gate_sigma * (1.0 + gate_act * (1.0 - gate_sigma))).astype(jnp.bfloat16)
    term_gate = jnp.dot(normal2.T, grad_gate, preferred_element_type=jnp.float32)
    term_up = jnp.dot(normal2.T, grad_up, preferred_element_type=jnp.float32)
    grad_norm2 = jnp.dot(grad_gate, full_gate.T, preferred_element_type=jnp.float32) + jnp.dot(grad_up, full_up.T, preferred_element_type=jnp.float32)
    normed_out, pull_second = jax.vjp(normed, resid2, gain_second)
    grad_part2, term_gain2 = pull_second(grad_norm2)
    grad_resid2 = grad_rows.astype(jnp.float32) + grad_part2
    grad_branch = grad_resid2.astype(jnp.bfloat16)
    term_out = jnp.dot(attended_rows.T, grad_branch, preferred_element_type=jnp.float32)
    grad_attended = jnp.dot(grad_branch, full_out.T, preferred_element_type=jnp.float32).astype(jnp.bfloat16)
    grad_grouped = grad_attended.reshape(LENGTH, KV_HEADS, repeat_count, HEAD)
    grad_query_acc, grad_keys_acc, grad_values_acc = attention_backward(query_grouped, key_rows, value_rows, attended, logsum, grad_grouped)
    grad_query = unrotate(grad_query_acc, cosine, sine_table).reshape(LENGTH, HEADS * HEAD).astype(jnp.bfloat16)
    grad_keys = unrotate(grad_keys_acc, cosine, sine_table).reshape(LENGTH, KV_HEADS * HEAD).astype(jnp.bfloat16)
    grad_values = grad_values_acc.reshape(LENGTH, KV_HEADS * HEAD).astype(jnp.bfloat16)
    term_query = jnp.dot(normal1.T, grad_query, preferred_element_type=jnp.float32)
    term_key = jnp.dot(normal1.T, grad_keys, preferred_element_type=jnp.float32)
    term_value = jnp.dot(normal1.T, grad_values, preferred_element_type=jnp.float32)
    grad_norm1 = jnp.dot(grad_query, full_query.T, preferred_element_type=jnp.float32)
    grad_norm1 = grad_norm1 + jnp.dot(grad_keys, full_key.T, preferred_element_type=jnp.float32)
    grad_norm1 = grad_norm1 + jnp.dot(grad_values, full_value.T, preferred_element_type=jnp.float32)
    normed_first, pull_first = jax.vjp(normed, resid1, gain_first)
    grad_part1, term_gain1 = pull_first(grad_norm1)
    grad_input = (grad_resid2 + grad_part1).astype(jnp.bfloat16)
    terms = (term_query, term_key, term_value, term_out, term_gate, term_up, term_down, term_gain1, term_gain2)
    return (output, grad_input, terms)

def reference(inputs, grad_output, w_query, w_key, w_value, w_out, w_gate, w_up, w_down, gain_attn, gain_mlp):
    weights = (w_query, w_key, w_value, w_out, w_gate, w_up, w_down)
    gains = (gain_attn.astype(jnp.float32), gain_mlp.astype(jnp.float32))
    zero_sums = tuple((jnp.zeros(matrix.shape, jnp.float32) for matrix in weights))
    zero_sums = zero_sums + (jnp.zeros((D,), jnp.float32), jnp.zeros((D,), jnp.float32))

    def seq_step(running, seq_pair):
        output, grad_input, terms = one_sequence(seq_pair[0], seq_pair[1], weights, gains)
        return (tuple((left + right for left, right in zip(running, terms))), (output, grad_input))
    totals, (outputs, grads) = lax.scan(seq_step, zero_sums, (inputs, grad_output))
    return (outputs, grads, totals[0], totals[1], totals[2], totals[3], totals[4], totals[5], totals[6], totals[7], totals[8])
```

```python
import jax
import jax.numpy as jnp
from jax import lax
from jax.sharding import PartitionSpec as P

HEADS = 15
KV_HEADS = 5
HEAD = 64


EPSILON = 1e-05
ROPE_THETA = 100000.0


def tables(positions, head_size):
    half_size = head_size // 2
    frequency = ROPE_THETA ** (-jnp.arange(half_size, dtype=jnp.float32) * 2.0 / head_size)
    angles = positions.astype(jnp.float32)[:, None] * frequency[None, :]
    return (jnp.cos(angles), jnp.sin(angles))


def rotate(values, cosine, sine_table):
    half_size = values.shape[-1] // 2
    first_half = values[..., :half_size]
    second = values[..., half_size:]
    cosine = cosine[:, None, :]
    sine_table = sine_table[:, None, :]
    return jnp.concatenate(
        [first_half * cosine - second * sine_table, second * cosine + first_half * sine_table],
        axis=-1,
    )


def unrotate(values, cosine, sine_table):
    half_size = values.shape[-1] // 2
    first_half = values[..., :half_size]
    second = values[..., half_size:]
    cosine = cosine[:, None, :]
    sine_table = sine_table[:, None, :]
    return jnp.concatenate(
        [first_half * cosine + second * sine_table, second * cosine - first_half * sine_table],
        axis=-1,
    )


def normed(row_values, gain_vec):
    scale_rows = lax.rsqrt(jnp.mean(row_values * row_values, axis=-1, keepdims=True) + EPSILON)
    return row_values * scale_rows * gain_vec


BOTH = ("fsdp", "ctx")


def forward_dot(pieces, halves):
    total = None
    for piece, half in zip(pieces, halves):
        term = lax.dot_general(
            piece, half, (((1,), (1,)), ((), ())), preferred_element_type=jnp.float32
        )
        total = term if total is None else total + term
    return total


def backward_dot(grads, halves):
    return jnp.concatenate(
        [jnp.dot(grads, half, preferred_element_type=jnp.float32) for half in halves], axis=-1
    )


def weight_terms(grads, pieces, cycle_size):
    terms = [
        lax.dot_general(
            grads, piece, (((0,), (0,)), ((), ())), preferred_element_type=jnp.float32
        ).astype(jnp.bfloat16)
        for piece in pieces
    ]
    return jnp.stack(
        [term.reshape(cycle_size, term.shape[0] // cycle_size, term.shape[1]) for term in terms]
    )


def cut(rows, count):
    return jnp.split(rows, count, axis=-1)


def gather_rows(packed, split_count, cycle_size):
    gathered = lax.all_gather(packed, BOTH, axis=0, tiled=False)
    return gathered.reshape(split_count, cycle_size, *packed.shape)


def take(gathered, start, size):
    piece = lax.slice_in_dim(gathered, start, start + size, axis=2)
    return [part.reshape(-1, part.shape[-1]) for part in piece]


def scatter_rows(terms):
    merged = terms.reshape(-1, *terms.shape[2:])
    return lax.psum_scatter(merged, BOTH, scatter_dimension=0, tiled=True)[0].astype(jnp.float32)


def local(
    inputs, grad_output, w_query, w_key, w_value, w_out, w_gate, w_up, w_down, gain_attn, gain_mlp
):
    seq_count, block_len, model_width = inputs.shape
    row_count = seq_count * block_len
    split_count = lax.axis_size("fsdp")
    cycle_size = lax.axis_size("ctx")
    cycle_index = lax.axis_index("ctx")
    length = block_len * cycle_size
    key_block = min(512, length)
    groups = KV_HEADS
    head_size = HEAD
    repeat_count = HEADS // KV_HEADS
    kv_width = groups * head_size
    positions = cycle_index * block_len + jnp.arange(block_len, dtype=jnp.int32)
    cosine, sine_table = tables(positions, head_size)
    cosine = jnp.tile(cosine, (seq_count, 1))
    sine_table = jnp.tile(sine_table, (seq_count, 1))
    needed = (cycle_index * block_len + block_len + key_block - 1) // key_block
    wide_q, wide_k, wide_v = w_query.shape[1], w_key.shape[1], w_value.shape[1]
    wide_o, wide_g, wide_u = w_out.shape[1], w_gate.shape[1], w_up.shape[1]
    part_width = w_query.shape[0]
    gain_size = gain_attn.shape[0]
    gain_row = jnp.pad(
        jnp.concatenate([gain_attn, gain_mlp]), (0, part_width - 2 * gain_size)
    )[None, :]
    packed_first = jnp.concatenate([w_query.T, w_key.T, w_value.T, gain_row], axis=0)
    packed_rest = jnp.concatenate([w_out.T, w_gate.T, w_up.T], axis=0)
    first = gather_rows(packed_first, split_count, cycle_size)
    rest = gather_rows(packed_rest, split_count, cycle_size)
    down = gather_rows(w_down.T, split_count, cycle_size)
    full_query = take(first, 0, wide_q)
    full_key = take(first, wide_q, wide_k)
    full_value = take(first, wide_q + wide_k, wide_v)
    gain_rows = first[0, :, wide_q + wide_k + wide_v, :]
    gain_first = gain_rows[:, :gain_size].reshape(-1).astype(jnp.float32)
    gain_second = gain_rows[:, gain_size : 2 * gain_size].reshape(-1).astype(jnp.float32)
    full_out = take(rest, 0, wide_o)
    full_gate = take(rest, wide_o, wide_g)
    full_up = take(rest, wide_o + wide_g, wide_u)
    full_down = take(down, 0, w_down.shape[1])

    resid1 = inputs.reshape(row_count, model_width).astype(jnp.float32)
    normal1 = normed(resid1, gain_first).astype(jnp.bfloat16)
    normal1_parts = cut(normal1, split_count)
    query_raw = forward_dot(normal1_parts, full_query).reshape(row_count, HEADS, head_size)
    query_rot = rotate(query_raw, cosine, sine_table).astype(jnp.bfloat16)
    key_raw = forward_dot(normal1_parts, full_key).reshape(row_count, groups, head_size)
    key_rows = (
        rotate(key_raw, cosine, sine_table)
        .astype(jnp.bfloat16)
        .reshape(seq_count, block_len, kv_width)
    )
    value_rows = (
        forward_dot(normal1_parts, full_value)
        .astype(jnp.bfloat16)
        .reshape(seq_count, block_len, kv_width)
    )
    query_grouped = query_rot.reshape(seq_count, block_len, groups, repeat_count, head_size)
    pair_all = lax.all_gather(
        jnp.concatenate([key_rows, value_rows], axis=-1), "ctx", axis=1, tiled=True
    )
    keys_all = pair_all[..., :kv_width]
    values_all = pair_all[..., kv_width:]
    key_heads = keys_all.reshape(seq_count, length, groups, head_size)
    value_heads = values_all.reshape(seq_count, length, groups, head_size)
    scores = (
        jnp.einsum(
            "sqgrd,skgd->sgrqk", query_grouped, key_heads, preferred_element_type=jnp.float32
        )
        * 0.125
    )
    allowed = jnp.arange(length, dtype=jnp.int32)[None, :] <= positions[:, None]
    scores = jnp.where(allowed, scores, -jnp.inf)
    new_peak = jnp.max(scores, axis=-1)
    exp_terms = jnp.exp(scores - new_peak[..., None])
    denom_run = jnp.sum(exp_terms, axis=-1)
    running = jnp.einsum(
        "sgrqk,skgd->sgrqd",
        exp_terms.astype(jnp.bfloat16),
        value_heads,
        preferred_element_type=jnp.float32,
    )
    attended_wide = running / denom_run[..., None]
    attended = jnp.transpose(attended_wide, (0, 3, 1, 2, 4)).astype(jnp.bfloat16)
    logsum = new_peak + jnp.log(denom_run)
    attended_rows = attended.reshape(row_count, HEADS * head_size)
    attended_parts = cut(attended_rows, split_count)
    resid2 = resid1 + forward_dot(attended_parts, full_out)
    normal2 = normed(resid2, gain_second).astype(jnp.bfloat16)
    normal2_parts = cut(normal2, split_count)
    gate_act = forward_dot(normal2_parts, full_gate)
    up_act = forward_dot(normal2_parts, full_up)
    gate_sigma = jax.nn.sigmoid(gate_act)
    hidden = (gate_act * gate_sigma * up_act).astype(jnp.bfloat16)
    hidden_parts = cut(hidden, split_count)
    output = (resid2 + forward_dot(hidden_parts, full_down)).astype(jnp.bfloat16)

    grad_rows = grad_output.reshape(row_count, model_width)
    sum_down = scatter_rows(weight_terms(grad_rows, hidden_parts, cycle_size))
    grad_hidden = backward_dot(grad_rows, full_down)
    grad_up = (grad_hidden * gate_act * gate_sigma).astype(jnp.bfloat16)
    grad_gate = (grad_hidden * up_act * gate_sigma * (1.0 + gate_act * (1.0 - gate_sigma))).astype(
        jnp.bfloat16
    )
    grad_norm2 = backward_dot(grad_gate, full_gate) + backward_dot(grad_up, full_up)
    normed_out, pull_second = jax.vjp(normed, resid2, gain_second)
    grad_part2, term_gain2 = pull_second(grad_norm2)
    grad_resid2 = grad_rows.astype(jnp.float32) + grad_part2
    grad_branch = grad_resid2.astype(jnp.bfloat16)
    sum_rest = scatter_rows(
        jnp.concatenate(
            [
                weight_terms(grad_branch, attended_parts, cycle_size),
                weight_terms(grad_gate, normal2_parts, cycle_size),
                weight_terms(grad_up, normal2_parts, cycle_size),
            ],
            axis=2,
        )
    )
    grad_attended = backward_dot(grad_branch, full_out).astype(jnp.bfloat16)
    grad_grouped = grad_attended.reshape(seq_count, block_len, groups, repeat_count, head_size)
    row_delta = jnp.sum(
        jnp.transpose(grad_grouped, (0, 2, 3, 1, 4)).astype(jnp.float32) * attended_wide, axis=-1
    )

    def retrace(step_index, loop_state):
        grad_query_acc, grad_pair_all = loop_state
        key_start = step_index * key_block
        pair = lax.dynamic_slice_in_dim(pair_all, key_start, key_block, 1)
        key_heads = pair[..., :kv_width].reshape(seq_count, key_block, groups, head_size)
        value_heads = pair[..., kv_width:].reshape(seq_count, key_block, groups, head_size)
        scores = (
            jnp.einsum(
                "sqgrd,skgd->sgrqk", query_grouped, key_heads, preferred_element_type=jnp.float32
            )
            * 0.125
        )
        allowed = (key_start + jnp.arange(key_block, dtype=jnp.int32))[None, :] <= positions[
            :, None
        ]
        prob_full = jnp.where(allowed, jnp.exp(jnp.where(allowed, scores, -jnp.inf) - logsum[..., None]), 0.0)
        grad_probs = jnp.einsum(
            "sqgrd,skgd->sgrqk", grad_grouped, value_heads, preferred_element_type=jnp.float32
        )
        grad_scores = (prob_full * (grad_probs - row_delta[..., None]) * 0.125).astype(jnp.bfloat16)
        prob_low = prob_full.astype(jnp.bfloat16)
        value_term = jnp.einsum(
            "sgrqk,sqgrd->skgd", prob_low, grad_grouped, preferred_element_type=jnp.float32
        ).reshape(seq_count, key_block, kv_width)
        key_term = jnp.einsum(
            "sgrqk,sqgrd->skgd", grad_scores, query_grouped, preferred_element_type=jnp.float32
        ).reshape(seq_count, key_block, kv_width)
        grad_query_acc = grad_query_acc + jnp.einsum(
            "sgrqk,skgd->sgrqd", grad_scores, key_heads, preferred_element_type=jnp.float32
        )
        pair_term = jnp.concatenate([key_term, value_term], axis=-1).astype(jnp.bfloat16)
        grad_pair_all = lax.dynamic_update_slice_in_dim(grad_pair_all, pair_term, key_start, 1)
        return (grad_query_acc, grad_pair_all)

    back_state = (
        jnp.zeros((seq_count, groups, repeat_count, block_len, head_size), jnp.float32),
        jnp.zeros((seq_count, length, 2 * kv_width), jnp.bfloat16),
    )
    grad_query_acc, grad_pair_all = lax.fori_loop(0, needed, retrace, back_state)
    grad_pair_own = lax.psum_scatter(
        grad_pair_all, "ctx", scatter_dimension=1, tiled=True
    ).astype(jnp.float32)
    grad_query_rows = jnp.transpose(grad_query_acc, (0, 3, 1, 2, 4)).reshape(
        row_count, HEADS, head_size
    )
    grad_query = (
        unrotate(grad_query_rows, cosine, sine_table)
        .reshape(row_count, HEADS * head_size)
        .astype(jnp.bfloat16)
    )
    grad_keys = (
        unrotate(
            grad_pair_own[..., :kv_width].reshape(row_count, groups, head_size), cosine, sine_table
        )
        .reshape(row_count, kv_width)
        .astype(jnp.bfloat16)
    )
    grad_values = grad_pair_own[..., kv_width:].reshape(row_count, kv_width).astype(jnp.bfloat16)
    grad_norm1 = backward_dot(grad_query, full_query)
    grad_norm1 = grad_norm1 + backward_dot(grad_keys, full_key)
    grad_norm1 = grad_norm1 + backward_dot(grad_values, full_value)
    normed_first, pull_first = jax.vjp(normed, resid1, gain_first)
    grad_part1, term_gain1 = pull_first(grad_norm1)
    grad_input = (
        (grad_resid2 + grad_part1).astype(jnp.bfloat16).reshape(seq_count, block_len, model_width)
    )
    gain_terms = jnp.concatenate(
        [term_gain1.reshape(cycle_size, -1), term_gain2.reshape(cycle_size, -1)], axis=-1
    ).astype(jnp.bfloat16)
    gain_terms = jnp.pad(gain_terms, ((0, 0), (0, part_width - 2 * gain_size)))
    gain_terms = jnp.broadcast_to(
        gain_terms[None, :, None, :], (split_count, cycle_size, 1, part_width)
    )
    sum_first = scatter_rows(
        jnp.concatenate(
            [
                weight_terms(grad_query, normal1_parts, cycle_size),
                weight_terms(grad_keys, normal1_parts, cycle_size),
                weight_terms(grad_values, normal1_parts, cycle_size),
                gain_terms,
            ],
            axis=2,
        )
    )
    gain_sums = sum_first[wide_q + wide_k + wide_v]
    return (
        output.reshape(seq_count, block_len, model_width),
        grad_input,
        sum_first[:wide_q].T,
        sum_first[wide_q : wide_q + wide_k].T,
        sum_first[wide_q + wide_k : wide_q + wide_k + wide_v].T,
        sum_rest[:wide_o].T,
        sum_rest[wide_o : wide_o + wide_g].T,
        sum_rest[wide_o + wide_g : wide_o + wide_g + wide_u].T,
        sum_down.T,
        gain_sums[:gain_size],
        gain_sums[gain_size : 2 * gain_size],
    )


def solution(mesh):
    return jax.shard_map(
        local,
        mesh=mesh,
        in_specs=(
            P("fsdp", "ctx", None),
            P("fsdp", "ctx", None),
            P("fsdp", "ctx"),
            P("fsdp", "ctx"),
            P("fsdp", "ctx"),
            P("fsdp", "ctx"),
            P("fsdp", "ctx"),
            P("fsdp", "ctx"),
            P("fsdp", "ctx"),
            P("ctx"),
            P("ctx"),
        ),
        out_specs=(
            P("fsdp", "ctx", None),
            P("fsdp", "ctx", None),
            P("fsdp", "ctx"),
            P("fsdp", "ctx"),
            P("fsdp", "ctx"),
            P("fsdp", "ctx"),
            P("fsdp", "ctx"),
            P("fsdp", "ctx"),
            P("fsdp", "ctx"),
            P("ctx"),
            P("ctx"),
        ),
        check_vma=False,
    )
```
